128 devices in a mesh: row: 8 (over y_hi, x), col: 16 (over y_lo, z, core).
Axes of the slice: x: 4, y: 4 (y_hi: 2, y_lo: 2; y = y_hi * 2 + y_lo), z: 4, core: 2. Of those that a mesh axis runs over, the one named last changes fastest.
Arguments:
- amplitudes: bfloat16 [6144, 63488], P('col', 'row'), may hold values from -6 to 6
- integrals: bfloat16 [63488, 256], P(('row', 'col')), may hold values from -0.09375 to 0.09375
- cd_irrep: int32 [496], P('row'), may hold values from 0 to 3
- ab_irrep: int32 [4], replicated, may hold values from 0 to 3
- pair_energy: float32 [6144], P('col'), may hold values from -2 to -0.5
- panel_energy: float32 [256], replicated, may hold values from 2 to 6
Outputs:
- update: bfloat16 [6144, 256], P('col', 'row')
The draws below stay inside these ranges and needn't reach their ends.
All inputs are finite; a program needn't handle non-finite values.
Results may differ from the reference program's by a relative error of at most 0.001.
Values may be sent and summed in bfloat16 or wider, within the bound.
No kernel may reach another device: no remote copies, remote signals or barrier semaphores. Data moves between devices by JAX's collectives and lax.ppermute only.
A program may use at most 64 MiB of HBM per device.

```python
import jax
import jax.numpy as jnp

PANEL = 256
KBLK = 128
ABLK = 64
PAIRS = 6144
CDPAIRS = 63488


def place_ends(entries, own_key, least, largest):
    shape = entries.shape
    place = [jax.random.randint(jax.random.fold_in(own_key, axis), (), 0, shape[axis]) for axis in range(len(shape))]
    entries = entries.at[tuple(place)].set(least)
    longest = shape.index(max(shape))
    place[longest] = (place[longest] + 1) % shape[longest]
    return entries.at[tuple(place)].set(largest)


def block_levels(rng, extent, shards, least, largest):
    level, own = 1.0, jax.random.fold_in(rng, 6)
    for dim, parts in shards:
        steps = jnp.exp(jax.random.uniform(jax.random.fold_in(own, dim), (parts,), jnp.float32, least / len(shards), largest / len(shards)))
        level = level * jnp.repeat(steps, extent[dim] // parts).reshape([-1 if axis == dim else 1 for axis in range(len(extent))])
    return level


def centred(own_key, dims, spread, bound, cuts=(), dtype=jnp.bfloat16):
    factor_of = block_levels(own_key, dims, cuts, -0.22, 0.18) if cuts else 1.0
    entries = jax.random.normal(own_key, dims, jnp.float32) * spread * factor_of
    return jnp.minimum(jnp.maximum(entries, -bound), bound).astype(dtype)


def setup_inputs(seed: int = 0) -> dict:
    seeds = jax.random.split(jax.random.key(seed), 7)
    return {
        "amplitudes": centred(seeds[0], (PAIRS, CDPAIRS), 1.0, 6.0, ((0, 16), (1, 8))),
        "integrals": centred(seeds[1], (CDPAIRS, PANEL), (CDPAIRS // 16) ** -0.5, 0.09375, ((0, 128),)),
        "cd_irrep": place_ends(jax.random.randint(seeds[2], (CDPAIRS // KBLK,), 0, 4), jax.random.fold_in(seeds[2], 1), 0, 3).astype(jnp.int32),
        "ab_irrep": place_ends(jax.random.randint(seeds[3], (PANEL // ABLK,), 0, 4), jax.random.fold_in(seeds[3], 1), 0, 3).astype(jnp.int32),
        "pair_energy": jnp.clip(-2.0 + 1.5 * jax.random.uniform(seeds[4], (PAIRS,), jnp.float32) ** block_levels(seeds[4], (PAIRS,), ((0, 16),), -0.2, 0.2), -2.0, -0.5),
        "panel_energy": jnp.clip(jax.random.uniform(seeds[5], (PANEL,), jnp.float32, 2.0, 6.0), 2.0, 6.0),
    }


def reference(amplitudes, integrals, cd_irrep, ab_irrep, pair_energy, panel_energy):
    labels = jnp.repeat(cd_irrep, KBLK)
    columns = jnp.repeat(ab_irrep, ABLK)
    masked = jnp.where(labels[:, None] == columns[None, :], integrals, jnp.zeros_like(integrals))
    ladder = jnp.dot(amplitudes, masked, preferred_element_type=jnp.float32)
    denom = panel_energy[None, :] - pair_energy[:, None]
    return (ladder / denom).astype(jnp.bfloat16)
```

```python
import functools

import jax
import jax.numpy as jnp
from jax import lax
from jax.experimental import pallas as pl
from jax.experimental.pallas import tpu as pltpu
from jax.sharding import PartitionSpec as P

KBLK = 128
ABLK = 64
SUB = 16
LANES = 128
VMEM = pltpu.VMEM
SMEM = pltpu.SMEM


def swap_halves(x):
    return jnp.concatenate([x[:, ABLK:], x[:, :ABLK]], axis=1)


def selectors(ab_ref, base):
    lane = lax.broadcasted_iota(jnp.int32, (1, LANES), 1)
    low = lane < ABLK
    rank = []
    for b in range(4):
        count = jnp.int32(-base)
        for earlier in range(b):
            count = count + jnp.where(ab_ref[earlier] == ab_ref[b], 1, 0)
        rank.append(count)
    rows = []
    for t in range(2):
        label = jnp.where(low, ab_ref[2 * t], ab_ref[2 * t + 1])
        slot = jnp.where(low, rank[2 * t], rank[2 * t + 1])
        half = jnp.where(low, 0, 1)
        rows.append((label, slot == half, slot == 1 - half))
    return rows


def factors(row, label):
    own, same, other = row
    match = own == label
    one = lambda m: jnp.where(m, 1.0, 0.0).astype(jnp.bfloat16)
    return one(match & same), one(match & other)


def pack_kernel(base, cd_ref, ab_ref, place_ref, v_ref, o_ref):
    rows = selectors(ab_ref, base)
    subs = v_ref.shape[0] // SUB
    first = place_ref[0] * subs
    for j in range(subs):
        label = cd_ref[(first + j) // (KBLK // SUB)]
        straight = crossed = None
        for t in range(2):
            x = v_ref[j * SUB:(j + 1) * SUB, t * LANES:(t + 1) * LANES]
            same, other = factors(rows[t], label)
            s, c = x * same, x * other
            straight = s if straight is None else straight + s
            crossed = c if crossed is None else crossed + c
        o_ref[j * SUB:(j + 1) * SUB, :] = straight + swap_halves(crossed)


def ladder_kernel(base, cd_ref, ab_ref, place_ref, t_ref, own_ref, other_ref, o_ref, held, masked):
    core = lax.rem(place_ref[0], 2)
    shards = 8
    depth = own_ref.shape[0] // shards
    for k in range(shards):
        for ref, c in ((own_ref, core), (other_ref, 1 - core)):
            at = pl.multiple_of((2 * k + c) * depth, SUB)
            held[pl.ds(at, depth), :] = ref[k * depth:(k + 1) * depth, :]
    rows = selectors(ab_ref, base)
    for blk in range(held.shape[0] // KBLK):
        x = held[blk * KBLK:(blk + 1) * KBLK, :]
        y = swap_halves(x)
        for t in range(2):
            same, other = factors(rows[t], cd_ref[blk])
            masked[blk * KBLK:(blk + 1) * KBLK, t * LANES:(t + 1) * LANES] = x * same + y * other
    total = jnp.dot(t_ref[...], masked[...], preferred_element_type=jnp.float32)
    o_ref[...] = total.T


SAME_CORE = [[2 * i + c for i in range(8)] for c in range(2)]
Z_GROUPS = [[y * 8 + z * 2 + c for z in range(4)] for y in range(2) for c in range(2)]
Y_GROUPS = [[y * 8 + z * 2 + c for y in range(2)] for z in range(4) for c in range(2)]
CORE_SWAP = [(i, i ^ 1) for i in range(16)]
SPREAD = "ag"


def partial_ladder(base, amplitudes, integrals, cd_irrep, ab_irrep, place):
    smem, vmem = pl.BlockSpec(memory_space=SMEM), pl.BlockSpec(memory_space=VMEM)
    depth, width = integrals.shape
    packed = pl.pallas_call(
        functools.partial(pack_kernel, base),
        out_shape=jax.ShapeDtypeStruct((depth, LANES), jnp.bfloat16),
        in_specs=[smem, smem, smem, vmem],
        out_specs=vmem,
        name="pack",
    )(cd_irrep, ab_irrep, place, integrals)
    if SPREAD == "ag":
        own = lax.all_gather(packed, "col", axis=0, tiled=True, axis_index_groups=Y_GROUPS)
        own = lax.all_gather(own.reshape(2, depth, LANES), "col", axis=1, tiled=True, axis_index_groups=Z_GROUPS).reshape(8 * depth, LANES)
    else:
        own = lax.all_to_all(jnp.broadcast_to(packed[None], (8, depth, LANES)), "col", 0, 0, tiled=True, axis_index_groups=SAME_CORE).reshape(8 * depth, LANES)
    other = lax.ppermute(own, "col", CORE_SWAP)
    ij = amplitudes.shape[0]
    cds = amplitudes.shape[1]
    return pl.pallas_call(
        functools.partial(ladder_kernel, base),
        out_shape=jax.ShapeDtypeStruct((width, ij), jnp.float32),
        in_specs=[smem, smem, smem, vmem, vmem, vmem],
        out_specs=vmem,
        scratch_shapes=[VMEM((cds, LANES), jnp.bfloat16), VMEM((cds, width), jnp.bfloat16)],
        compiler_params=pltpu.CompilerParams(vmem_limit_bytes=60 * 2**20),
        cost_estimate=pl.CostEstimate(flops=2 * ij * cds * width, bytes_accessed=2 * ij * cds, transcendentals=0),
        name="ladder",
    )(cd_irrep, ab_irrep, place, amplitudes, own, other)


def shards(amplitudes, integrals, cd_irrep, ab_irrep, pair_energy, panel_energy):
    place = lax.axis_index("col").astype(jnp.int32).reshape(1)
    args = (amplitudes, integrals, cd_irrep, ab_irrep, place)
    partial_sum = partial_ladder(0, *args)
    most = jnp.max(jnp.sum(ab_irrep[:, None] == ab_irrep[None, :], axis=0))
    partial_sum = lax.cond(most > 2, lambda p, *a: p + partial_ladder(2, *a), lambda p, *a: p, partial_sum, *args)
    width = partial_sum.shape[0]
    row_count = lax.axis_size("row")
    share = width // row_count
    parts = lax.all_to_all(partial_sum, "row", 0, 0, tiled=True)
    summed = jnp.sum(parts.reshape(row_count, share, -1), axis=0)
    energy_cols = lax.dynamic_slice_in_dim(panel_energy, lax.axis_index("row") * share, share, 0)
    denom = energy_cols[:, None] - pair_energy[None, :]
    return (summed / denom).astype(jnp.bfloat16).T


def solution(mesh):
    in_specs = (P("col", "row"), P(("row", "col"), None), P("row"), P(), P("col"), P())
    out_specs = P("col", "row")
    return jax.shard_map(shards, mesh=mesh, in_specs=in_specs, out_specs=out_specs, check_vma=False)
```

```python
import functools

import jax
import jax.numpy as jnp
from jax import lax
from jax.experimental import pallas as pl
from jax.experimental.pallas import tpu as pltpu
from jax.sharding import PartitionSpec as P


KBLK = 128
ABLK = 64
SUB = 16
LANES = 128
LABELS = 4
VMEM = pltpu.VMEM
SMEM = pltpu.SMEM
IN_SMEM = pl.BlockSpec(memory_space=SMEM)
IN_VMEM = pl.BlockSpec(memory_space=VMEM)


def swap_halves(x):
    return jnp.concatenate([x[:, ABLK:], x[:, :ABLK]], axis=1)


def ranks(ab_ref, base):
    out = []
    for b in range(4):
        count = jnp.int32(-base)
        for earlier in range(b):
            count = count + jnp.where(ab_ref[earlier] == ab_ref[b], 1, 0)
        out.append(count)
    return out


def fill_factors(ab_ref, base, table):
    lane = lax.broadcasted_iota(jnp.int32, (SUB, LANES), 1)
    low = lane < ABLK
    rank = ranks(ab_ref, base)
    for t in range(2):
        own = jnp.where(low, ab_ref[2 * t], ab_ref[2 * t + 1])
        slot = jnp.where(low, rank[2 * t], rank[2 * t + 1])
        half = jnp.where(low, 0, 1)
        for label in range(LABELS):
            for kind, want in enumerate((half, 1 - half)):
                hit = jnp.where(own == label, jnp.where(slot == want, 1.0, 0.0), 0.0)
                table[(label * 2 + t) * 2 + kind] = hit.astype(jnp.bfloat16)


def half_of(t_ref, place_ref, dy, dst, sem):
    cols = dst.shape[1]
    at = pl.multiple_of(half_place(place_ref, dy) * cols, LANES)
    return pltpu.make_async_copy(t_ref.at[:, pl.ds(at, cols)], dst, sem)


def pack_kernel(base, cd_ref, ab_ref, place_ref, v_ref, o_ref, most_ref, table):
    fill_factors(ab_ref, base, table)
    most = jnp.int32(0)
    for count in ranks(ab_ref, 0):
        most = jnp.maximum(most, count)
    most_ref[0] = most + 1
    subs = v_ref.shape[0] // SUB
    first = place_ref[0] * subs
    for j in range(subs):
        label = cd_ref[(first + j) // (KBLK // SUB)]
        straight = crossed = None
        for t in range(2):
            x = v_ref[j * SUB:(j + 1) * SUB, t * LANES:(t + 1) * LANES]
            s, c = x * table[label * 4 + t * 2], x * table[label * 4 + t * 2 + 1]
            straight = s if straight is None else straight + s
            crossed = c if crossed is None else crossed + c
        o_ref[j * SUB:(j + 1) * SUB, :] = straight + swap_halves(crossed)


def pack(base, cd_irrep, ab_irrep, place, integrals):
    return pl.pallas_call(
        functools.partial(pack_kernel, base),
        out_shape=(
            jax.ShapeDtypeStruct((integrals.shape[0], LANES), jnp.bfloat16),
            jax.ShapeDtypeStruct((1,), jnp.int32),
            jax.ShapeDtypeStruct((LABELS * 4, SUB, LANES), jnp.bfloat16),
        ),
        in_specs=[IN_SMEM, IN_SMEM, IN_SMEM, IN_VMEM],
        out_specs=(IN_VMEM, IN_SMEM, IN_VMEM),
        compiler_params=pltpu.CompilerParams(vmem_limit_bytes=2 * 2**20),
        name="pack",
    )(cd_irrep, ab_irrep, place, integrals)


def half_ladder(dy, cd_ref, place_ref, table, piece_refs, held, masked):
    col = place_ref[0]
    core, z = lax.rem(col, 2), lax.rem(col // 2, 4)
    half = half_place(place_ref, dy)
    depth = piece_refs[0].shape[0]
    for n, ref in enumerate(piece_refs):
        dz = STEPS[n % 4]
        from_core = core if n < 4 else 1 - core
        at = (lax.rem(z + 4 - dz, 4) * 2 + from_core) * depth
        held[pl.ds(pl.multiple_of(at, SUB), depth), :] = ref[...]
    blocks = held.shape[0] // KBLK
    for blk in range(blocks):
        at = slice(blk * KBLK, (blk + 1) * KBLK)
        x = held[at, :]
        y = swap_halves(x)
        label = cd_ref[half * blocks + blk]
        for t in range(2):
            same, other = [jnp.concatenate([table[label * 4 + t * 2 + kind]] * (KBLK // SUB), 0) for kind in range(2)]
            masked[at, t * LANES:(t + 1) * LANES] = x * same + y * other


def half_place(place_ref, dy):
    return lax.rem(place_ref[0] // 8 + dy, 2)


def fetch_kernel(place_ref, t_ref, block, rest, sems):
    copies = [half_of(t_ref, place_ref, dy, dst, sems.at[dy]) for dy, dst in enumerate((block, rest))]
    for copy in copies:
        copy.start()
    for copy in copies:
        copy.wait()


def first_kernel(cd_ref, place_ref, table, block, *refs):
    piece_refs = refs[:8]
    o_ref, held, masked = refs[8:]
    half_ladder(0, cd_ref, place_ref, table, piece_refs, held, masked)
    o_ref[...] = jnp.dot(block[...], masked[...], preferred_element_type=jnp.float32)


def last_kernel(cd_ref, place_ref, table, block, before_ref, *refs):
    piece_refs = refs[:8]
    o_ref, held, masked = refs[8:]
    half_ladder(1, cd_ref, place_ref, table, piece_refs, held, masked)
    o_ref[...] = (before_ref[...] + jnp.dot(block[...], masked[...], preferred_element_type=jnp.float32)).T


STEPS = (0, 2, 1, 3)
CORE_SWAP = [(i, i ^ 1) for i in range(16)]


def hop(dy, dz):
    return [(i, ((i // 8 ^ dy) * 4 + (i // 2 + dz) % 4) * 2 + i % 2) for i in range(16)]


def partial_ladder(packed, table, amplitudes, cd_irrep, place):
    across = lax.ppermute(packed, "col", hop(1, 0))
    pieces = []
    for start in (packed, across):
        mine = [start]
        for dz in STEPS[1:]:
            mine.append(lax.ppermute(start, "col", hop(0, dz)))
        theirs = []
        for dz, piece in zip(STEPS, mine):
            theirs.append(lax.ppermute(piece, "col", CORE_SWAP))
        pieces.append(mine + theirs)
    ij, cds = amplitudes.shape
    width, cols = 2 * LANES, cds // 2
    scratch = [VMEM((cols, LANES), jnp.bfloat16), VMEM((cols, width), jnp.bfloat16)]
    cost = pl.CostEstimate(flops=ij * cds * width, bytes_accessed=ij * cds, transcendentals=0)
    limits = pltpu.CompilerParams(vmem_limit_bytes=12 * 2**20)
    block, rest = pl.pallas_call(
        fetch_kernel,
        out_shape=[jax.ShapeDtypeStruct((ij, cols), jnp.bfloat16)] * 2,
        in_specs=[IN_SMEM, pl.BlockSpec(memory_space=pl.ANY)],
        out_specs=[IN_VMEM] * 2,
        scratch_shapes=[pltpu.SemaphoreType.DMA((2,))],
        compiler_params=pltpu.CompilerParams(vmem_limit_bytes=8 * 2**20),
        cost_estimate=pl.CostEstimate(flops=0, bytes_accessed=2 * ij * cds, transcendentals=0),
        name="fetch",
    )(place, amplitudes)
    half = pl.pallas_call(
        first_kernel,
        out_shape=jax.ShapeDtypeStruct((ij, width), jnp.float32),
        in_specs=[IN_SMEM] * 2 + [IN_VMEM] * 10,
        out_specs=IN_VMEM,
        scratch_shapes=scratch,
        compiler_params=limits,
        cost_estimate=cost,
        name="ladder_first",
    )(cd_irrep, place, table, block, *pieces[0])
    return pl.pallas_call(
        last_kernel,
        out_shape=jax.ShapeDtypeStruct((width, ij), jnp.float32),
        in_specs=[IN_SMEM] * 2 + [IN_VMEM] * 11,
        out_specs=IN_VMEM,
        scratch_shapes=scratch,
        compiler_params=limits,
        cost_estimate=cost,
        name="ladder_last",
    )(cd_irrep, place, table, rest, half, *pieces[1])


def shards(amplitudes, integrals, cd_irrep, ab_irrep, pair_energy, panel_energy):
    place = lax.axis_index("col").astype(jnp.int32).reshape(1)
    packed, most, table = pack(0, cd_irrep, ab_irrep, place, integrals)
    partial_sum = partial_ladder(packed, table, amplitudes, cd_irrep, place)

    def more(p, amplitudes, integrals, cd_irrep, ab_irrep, place):
        rest, _, table = pack(2, cd_irrep, ab_irrep, place, integrals)
        return p + partial_ladder(rest, table, amplitudes, cd_irrep, place)

    partial_sum = lax.cond(most[0] > 2, more, lambda p, *a: p, partial_sum, amplitudes, integrals, cd_irrep, ab_irrep, place)
    width = partial_sum.shape[0]
    row_count = lax.axis_size("row")
    share = width // row_count
    parts = lax.all_to_all(partial_sum, "row", 0, 0, tiled=True)
    summed = jnp.sum(parts.reshape(row_count, share, -1), axis=0)
    energy_cols = lax.dynamic_slice_in_dim(panel_energy, lax.axis_index("row") * share, share, 0)
    denom = energy_cols[:, None] - pair_energy[None, :]
    return (summed / denom).astype(jnp.bfloat16).T


def solution(mesh):
    in_specs = (P("col", "row"), P(("row", "col"), None), P("row"), P(), P("col"), P())
    out_specs = P("col", "row")
    return jax.shard_map(shards, mesh=mesh, in_specs=in_specs, out_specs=out_specs, check_vma=False)
```

```python
import functools

import jax
import jax.numpy as jnp
from jax import lax
from jax.experimental import pallas as pl
from jax.experimental.pallas import tpu as pltpu
from jax.sharding import PartitionSpec as P


KBLK = 128
ABLK = 64
SUB = 16
LANES = 128
LABELS = 4
VMEM = pltpu.VMEM
SMEM = pltpu.SMEM
IN_SMEM = pl.BlockSpec(memory_space=SMEM)
IN_VMEM = pl.BlockSpec(memory_space=VMEM)


def swap_halves(x):
    return jnp.concatenate([x[:, ABLK:], x[:, :ABLK]], axis=1)


def ranks(ab_ref, base):
    out = []
    for b in range(4):
        count = jnp.int32(-base)
        for earlier in range(b):
            count = count + jnp.where(ab_ref[earlier] == ab_ref[b], 1, 0)
        out.append(count)
    return out


def fill_factors(ab_ref, base, table):
    lane = lax.broadcasted_iota(jnp.int32, (SUB, LANES), 1)
    low = lane < ABLK
    rank = ranks(ab_ref, base)
    for t in range(2):
        own = jnp.where(low, ab_ref[2 * t], ab_ref[2 * t + 1])
        slot = jnp.where(low, rank[2 * t], rank[2 * t + 1])
        half = jnp.where(low, 0, 1)
        for label in range(LABELS):
            for kind, want in enumerate((half, 1 - half)):
                hit = jnp.where(own == label, jnp.where(slot == want, 1.0, 0.0), 0.0)
                table[(label * 2 + t) * 2 + kind] = hit.astype(jnp.bfloat16)


def pack_kernel(base, cd_ref, ab_ref, place_ref, v_ref, o_ref, most_ref, table):
    fill_factors(ab_ref, base, table)
    most = jnp.int32(0)
    for count in ranks(ab_ref, 0):
        most = jnp.maximum(most, count)
    most_ref[0] = most + 1
    subs = v_ref.shape[0] // SUB
    first = place_ref[0] * subs
    for j in range(subs):
        label = cd_ref[(first + j) // (KBLK // SUB)]
        straight = crossed = None
        for t in range(2):
            x = v_ref[j * SUB:(j + 1) * SUB, t * LANES:(t + 1) * LANES]
            s, c = x * table[label * 4 + t * 2], x * table[label * 4 + t * 2 + 1]
            straight = s if straight is None else straight + s
            crossed = c if crossed is None else crossed + c
        o_ref[j * SUB:(j + 1) * SUB, :] = straight + swap_halves(crossed)


def pack(base, cd_irrep, ab_irrep, place, integrals):
    return pl.pallas_call(
        functools.partial(pack_kernel, base),
        out_shape=(
            jax.ShapeDtypeStruct((integrals.shape[0], LANES), jnp.bfloat16),
            jax.ShapeDtypeStruct((1,), jnp.int32),
            jax.ShapeDtypeStruct((LABELS * 4, SUB, LANES), jnp.bfloat16),
        ),
        in_specs=[IN_SMEM, IN_SMEM, IN_SMEM, IN_VMEM],
        out_specs=(IN_VMEM, IN_SMEM, IN_VMEM),
        compiler_params=pltpu.CompilerParams(vmem_limit_bytes=2 * 2**20),
        cost_estimate=pl.CostEstimate(flops=10**10, bytes_accessed=2 * integrals.size, transcendentals=0),
        name="pack",
    )(cd_irrep, ab_irrep, place, integrals)


def half_ladder(dy, cd_ref, place_ref, table, piece_refs, held, masked):
    col = place_ref[0]
    core, z = lax.rem(col, 2), lax.rem(col // 2, 4)
    half = half_place(place_ref, dy)
    depth = piece_refs[0].shape[0]
    for n, ref in enumerate(piece_refs):
        dz = STEPS[n % 4]
        from_core = core if n < 4 else 1 - core
        at = (lax.rem(z + 4 - dz, 4) * 2 + from_core) * depth
        held[pl.ds(pl.multiple_of(at, SUB), depth), :] = ref[...]
    blocks = held.shape[0] // KBLK
    for blk in range(blocks):
        at = slice(blk * KBLK, (blk + 1) * KBLK)
        x = held[at, :]
        y = swap_halves(x)
        label = cd_ref[half * blocks + blk]
        for t in range(2):
            same, other = [jnp.concatenate([table[label * 4 + t * 2 + kind]] * (KBLK // SUB), 0) for kind in range(2)]
            masked[at, t * LANES:(t + 1) * LANES] = x * same + y * other


def half_place(place_ref, dy):
    return lax.rem(place_ref[0] // 8 + dy, 2)


def half_product(dy, place_ref, t_ref, masked):
    depth = masked.shape[0]
    cols = pl.ds(pl.multiple_of(half_place(place_ref, dy) * depth, LANES), depth)
    return jnp.dot(t_ref[:, cols], masked[...], preferred_element_type=jnp.float32)


def first_kernel(cd_ref, place_ref, table, t_ref, *refs):
    piece_refs = refs[:8]
    o_ref, held, masked = refs[8:]
    half_ladder(0, cd_ref, place_ref, table, piece_refs, held, masked)
    o_ref[...] = half_product(0, place_ref, t_ref, masked)


def last_kernel(cd_ref, place_ref, table, t_ref, before_ref, *refs):
    piece_refs, out_refs = refs[:8], refs[8:16]
    held, masked, total = refs[16:]
    half_ladder(1, cd_ref, place_ref, table, piece_refs, held, masked)
    total[...] = (before_ref[...] + half_product(1, place_ref, t_ref, masked)).T
    row = place_ref[1]
    y, x = row // 4, lax.rem(row, 4)
    for (dy, dx), ref in zip(TARGETS, out_refs):
        target = lax.rem(y + dy, 2) * 4 + lax.rem(x + dx, 4)
        share = ref.shape[0]
        ref[...] = total[pl.ds(pl.multiple_of(target * share, 8), share), :]


TARGETS = [(0, 0), (1, 2), (1, 1), (1, 3), (1, 0), (0, 2), (0, 1), (0, 3)]


def row_hop(dy, dx):
    return [(i, (i // 4 ^ dy) * 4 + (i % 4 + dx) % 4) for i in range(8)]


def reduce_parts(blocks):
    parts = [blocks[0]]
    for n, block in enumerate(blocks[1:], 1):
        parts.append(lax.ppermute(block, "row", row_hop(*TARGETS[n])))
    return parts


STEPS = (0, 2, 1, 3)
CORE_SWAP = [(i, i ^ 1) for i in range(16)]


def hop(dy, dz):
    return [(i, ((i // 8 ^ dy) * 4 + (i // 2 + dz) % 4) * 2 + i % 2) for i in range(16)]


def partial_ladder(packed, table, amplitudes, cd_irrep, place):
    across = lax.ppermute(packed, "col", hop(1, 0))
    pieces = []
    for start in (packed, across):
        mine = [start]
        for dz in STEPS[1:]:
            mine.append(lax.ppermute(start, "col", hop(0, dz)))
        theirs = []
        for dz, piece in zip(STEPS, mine):
            theirs.append(lax.ppermute(piece, "col", CORE_SWAP))
        pieces.append(mine + theirs)
    ij, cds = amplitudes.shape
    width, cols = 2 * LANES, cds // 2
    scratch = [VMEM((cols, LANES), jnp.bfloat16), VMEM((cols, width), jnp.bfloat16)]
    cost = pl.CostEstimate(flops=ij * cds * width, bytes_accessed=ij * cds, transcendentals=0)
    limits = pltpu.CompilerParams(vmem_limit_bytes=12 * 2**20)
    half = pl.pallas_call(
        first_kernel,
        out_shape=jax.ShapeDtypeStruct((ij, width), jnp.float32),
        in_specs=[IN_SMEM] * 2 + [IN_VMEM] * 10,
        out_specs=IN_VMEM,
        scratch_shapes=scratch,
        compiler_params=limits,
        cost_estimate=cost,
        name="ladder_first",
    )(cd_irrep, place, table, amplitudes, *pieces[0])
    return pl.pallas_call(
        last_kernel,
        out_shape=[jax.ShapeDtypeStruct((width // 8, ij), jnp.float32)] * 8,
        in_specs=[IN_SMEM] * 2 + [IN_VMEM] * 11,
        out_specs=[IN_VMEM] * 8,
        scratch_shapes=scratch + [VMEM((width, ij), jnp.float32)],
        compiler_params=limits,
        cost_estimate=cost,
        name="ladder_last",
    )(cd_irrep, place, table, amplitudes, half, *pieces[1])


def shards(amplitudes, integrals, cd_irrep, ab_irrep, pair_energy, panel_energy):
    place = jnp.stack([lax.axis_index("col"), lax.axis_index("row")]).astype(jnp.int32)
    packed, most, table = pack(0, cd_irrep, ab_irrep, place, integrals)
    parts = reduce_parts(partial_ladder(packed, table, amplitudes, cd_irrep, place))

    def finish(parts, pair_energy, panel_energy):
        share = parts[0].shape[0]
        summed = sum(parts[1:], parts[0])
        energy_cols = lax.dynamic_slice_in_dim(panel_energy, lax.axis_index("row") * share, share, 0)
        denom = energy_cols[:, None] - pair_energy[None, :]
        return (summed / denom).astype(jnp.bfloat16).T

    def more(parts, pair_energy, panel_energy, amplitudes, integrals, cd_irrep, ab_irrep, place):
        rest, _, table = pack(2, cd_irrep, ab_irrep, place, integrals)
        extra = reduce_parts(partial_ladder(rest, table, amplitudes, cd_irrep, place))
        return finish([p + e for p, e in zip(parts, extra)], pair_energy, panel_energy)

    def enough(parts, pair_energy, panel_energy, *unused):
        return finish(parts, pair_energy, panel_energy)

    parts = lax.optimization_barrier(parts)
    operands = (parts, pair_energy, panel_energy, amplitudes, integrals, cd_irrep, ab_irrep, place)
    return lax.cond(most[0] > 2, more, enough, *operands)


def solution(mesh):
    in_specs = (P("col", "row"), P(("row", "col"), None), P("row"), P(), P("col"), P())
    out_specs = P("col", "row")
    return jax.shard_map(shards, mesh=mesh, in_specs=in_specs, out_specs=out_specs, check_vma=False)
```

```python
import jax
import jax.numpy as jnp
from jax import lax
from jax.experimental import pallas as pl
from jax.experimental.pallas import tpu as pltpu
from jax.sharding import PartitionSpec as P


KBLK = 128
ABLK = 64
SUB = 16
LANES = 128
LABELS = 4
KINDS = 3
VMEM = pltpu.VMEM
SMEM = pltpu.SMEM
IN_SMEM = pl.BlockSpec(memory_space=SMEM)
IN_VMEM = pl.BlockSpec(memory_space=VMEM)


def swap_halves(x):
    return jnp.concatenate([x[:, ABLK:], x[:, :ABLK]], axis=1)


def ranks(ab_ref):
    out = []
    for b in range(4):
        count = jnp.int32(0)
        for earlier in range(b):
            count = count + jnp.where(ab_ref[earlier] == ab_ref[b], 1, 0)
        out.append(count)
    return out


def fill_factors(ab_ref, table):
    lane = lax.broadcasted_iota(jnp.int32, (SUB, LANES), 1)
    low = lane < ABLK
    rank = ranks(ab_ref)
    for t in range(2):
        own = jnp.where(low, ab_ref[2 * t], ab_ref[2 * t + 1])
        slot = jnp.where(low, rank[2 * t], rank[2 * t + 1])
        half = jnp.where(low, 0, 1)
        for label in range(LABELS):
            for kind, want in enumerate((half, 1 - half)):
                hit = jnp.where(own == label, jnp.where(slot == want, 1.0, 0.0), 0.0)
                table[(label * 2 + t) * KINDS + kind] = hit.astype(jnp.bfloat16)
            table[(label * 2 + t) * KINDS + 2] = jnp.where(own == label, 1.0, 0.0).astype(jnp.bfloat16)


def pack_kernel(cd_ref, ab_ref, place_ref, v_ref, o_ref, most_ref, table):
    fill_factors(ab_ref, table)
    most = jnp.int32(0)
    for count in ranks(ab_ref):
        most = jnp.maximum(most, count)
    most_ref[0] = most + 1
    subs = v_ref.shape[0] // SUB
    first = place_ref[0] * subs
    for j in range(subs):
        label = cd_ref[(first + j) // (KBLK // SUB)]
        straight = crossed = None
        for t in range(2):
            x = v_ref[j * SUB:(j + 1) * SUB, t * LANES:(t + 1) * LANES]
            at = (label * 2 + t) * KINDS
            s, c = x * table[at], x * table[at + 1]
            straight = s if straight is None else straight + s
            crossed = c if crossed is None else crossed + c
        o_ref[j * SUB:(j + 1) * SUB, :] = straight + swap_halves(crossed)


def pack(cd_irrep, ab_irrep, place, integrals):
    return pl.pallas_call(
        pack_kernel,
        out_shape=(
            jax.ShapeDtypeStruct((integrals.shape[0], LANES), jnp.bfloat16),
            jax.ShapeDtypeStruct((1,), jnp.int32),
            jax.ShapeDtypeStruct((LABELS * 2 * KINDS, SUB, LANES), jnp.bfloat16),
        ),
        in_specs=[IN_SMEM, IN_SMEM, IN_SMEM, IN_VMEM],
        out_specs=(IN_VMEM, IN_SMEM, IN_VMEM),
        compiler_params=pltpu.CompilerParams(vmem_limit_bytes=2 * 2**20),
        cost_estimate=pl.CostEstimate(flops=10**10, bytes_accessed=2 * integrals.size, transcendentals=0),
        name="pack",
    )(cd_irrep, ab_irrep, place, integrals)


def half_ladder(dy, cd_ref, place_ref, table, piece_refs, held, masked):
    col = place_ref[0]
    core, z = lax.rem(col, 2), lax.rem(col // 2, 4)
    half = half_place(place_ref, dy)
    depth = piece_refs[0].shape[0]
    for n, ref in enumerate(piece_refs):
        dz = STEPS[n % 4]
        from_core = core if n < 4 else 1 - core
        at = (lax.rem(z + 4 - dz, 4) * 2 + from_core) * depth
        held[pl.ds(pl.multiple_of(at, SUB), depth), :] = ref[...]
    blocks = held.shape[0] // KBLK
    wide = held.shape[1] > LANES
    for blk in range(blocks):
        at = slice(blk * KBLK, (blk + 1) * KBLK)
        label = cd_ref[half * blocks + blk]
        for t in range(2):
            lanes = slice(t * LANES, (t + 1) * LANES)
            same, other, match = [jnp.concatenate([table[(label * 2 + t) * KINDS + kind]] * (KBLK // SUB), 0) for kind in range(3)]
            if wide:
                masked[at, lanes] = held[at, lanes] * match
            else:
                x = held[at, :]
                masked[at, lanes] = x * same + swap_halves(x) * other


def half_place(place_ref, dy):
    return lax.rem(place_ref[0] // 8 + dy, 2)


def half_product(dy, place_ref, t_ref, masked):
    depth = masked.shape[0]
    cols = pl.ds(pl.multiple_of(half_place(place_ref, dy) * depth, LANES), depth)
    return jnp.dot(t_ref[:, cols], masked[...], preferred_element_type=jnp.float32)


def first_kernel(cd_ref, place_ref, table, t_ref, *refs):
    piece_refs = refs[:8]
    o_ref, held, masked = refs[8:]
    half_ladder(0, cd_ref, place_ref, table, piece_refs, held, masked)
    o_ref[...] = half_product(0, place_ref, t_ref, masked)


def last_kernel(cd_ref, place_ref, table, t_ref, before_ref, *refs):
    piece_refs, out_refs = refs[:8], refs[8:16]
    held, masked, total = refs[16:]
    half_ladder(1, cd_ref, place_ref, table, piece_refs, held, masked)
    total[...] = (before_ref[...] + half_product(1, place_ref, t_ref, masked)).T
    row = place_ref[1]
    y, x = row // 4, lax.rem(row, 4)
    for (dy, dx), ref in zip(TARGETS, out_refs):
        target = lax.rem(y + dy, 2) * 4 + lax.rem(x + dx, 4)
        share = ref.shape[0]
        ref[...] = total[pl.ds(pl.multiple_of(target * share, 8), share), :]


TARGETS = [(0, 0), (1, 2), (1, 1), (1, 3), (1, 0), (0, 2), (0, 1), (0, 3)]


def row_hop(dy, dx):
    return [(i, (i // 4 ^ dy) * 4 + (i % 4 + dx) % 4) for i in range(8)]


def reduce_parts(blocks):
    parts = [blocks[0]]
    for n, block in enumerate(blocks[1:], 1):
        parts.append(lax.ppermute(block, "row", row_hop(*TARGETS[n])))
    return parts


STEPS = (0, 2, 1, 3)
CORE_SWAP = [(i, i ^ 1) for i in range(16)]


def hop(dy, dz):
    return [(i, ((i // 8 ^ dy) * 4 + (i // 2 + dz) % 4) * 2 + i % 2) for i in range(16)]


def partial_ladder(packed, table, amplitudes, cd_irrep, place):
    across = lax.ppermute(packed, "col", hop(1, 0))
    pieces = []
    for start in (packed, across):
        mine = [start]
        for dz in STEPS[1:]:
            mine.append(lax.ppermute(start, "col", hop(0, dz)))
        theirs = []
        for dz, piece in zip(STEPS, mine):
            theirs.append(lax.ppermute(piece, "col", CORE_SWAP))
        pieces.append(mine + theirs)
    ij, cds = amplitudes.shape
    width, cols = 2 * LANES, cds // 2
    scratch = [VMEM((cols, packed.shape[1]), jnp.bfloat16), VMEM((cols, width), jnp.bfloat16)]
    cost = pl.CostEstimate(flops=ij * cds * width, bytes_accessed=ij * cds, transcendentals=0)
    limits = pltpu.CompilerParams(vmem_limit_bytes=12 * 2**20)
    half = pl.pallas_call(
        first_kernel,
        out_shape=jax.ShapeDtypeStruct((ij, width), jnp.float32),
        in_specs=[IN_SMEM] * 2 + [IN_VMEM] * 10,
        out_specs=IN_VMEM,
        scratch_shapes=scratch,
        compiler_params=limits,
        cost_estimate=cost,
        name="ladder_first",
    )(cd_irrep, place, table, amplitudes, *pieces[0])
    return pl.pallas_call(
        last_kernel,
        out_shape=[jax.ShapeDtypeStruct((width // 8, ij), jnp.float32)] * 8,
        in_specs=[IN_SMEM] * 2 + [IN_VMEM] * 11,
        out_specs=[IN_VMEM] * 8,
        scratch_shapes=scratch + [VMEM((width, ij), jnp.float32)],
        compiler_params=limits,
        cost_estimate=cost,
        name="ladder_last",
    )(cd_irrep, place, table, amplitudes, half, *pieces[1])


def shards(amplitudes, integrals, cd_irrep, ab_irrep, pair_energy, panel_energy):
    place = jnp.stack([lax.axis_index("col"), lax.axis_index("row")]).astype(jnp.int32)
    packed, most, table = pack(cd_irrep, ab_irrep, place, integrals)

    def narrow(packed, integrals, *rest):
        return partial_ladder(packed, *rest)

    def whole(packed, integrals, *rest):
        return partial_ladder(integrals, *rest)

    blocks = lax.cond(most[0] > 2, whole, narrow, packed, integrals, table, amplitudes, cd_irrep, place)
    parts = reduce_parts(blocks)
    share = parts[0].shape[0]
    summed = sum(parts[1:], parts[0])
    energy_cols = lax.dynamic_slice_in_dim(panel_energy, lax.axis_index("row") * share, share, 0)
    denom = energy_cols[:, None] - pair_energy[None, :]
    return (summed / denom).astype(jnp.bfloat16).T


def solution(mesh):
    in_specs = (P("col", "row"), P(("row", "col"), None), P("row"), P(), P("col"), P())
    out_specs = P("col", "row")
    return jax.shard_map(shards, mesh=mesh, in_specs=in_specs, out_specs=out_specs, check_vma=False)
```

```python
import jax
import jax.numpy as jnp
from jax import lax
from jax.experimental import pallas as pl
from jax.experimental.pallas import tpu as pltpu
from jax.sharding import PartitionSpec as P


KBLK = 128
ABLK = 64
SUB = 16
LANES = 128
LABELS = 4
KINDS = 3
TABLE = pltpu.VMEM((LABELS * 2 * KINDS, SUB, LANES), jnp.bfloat16)
VMEM = pltpu.VMEM
SMEM = pltpu.SMEM
IN_SMEM = pl.BlockSpec(memory_space=SMEM)
IN_VMEM = pl.BlockSpec(memory_space=VMEM)


def swap_halves(x):
    return jnp.concatenate([x[:, ABLK:], x[:, :ABLK]], axis=1)


def ranks(ab_ref):
    out = []
    for b in range(4):
        count = jnp.int32(0)
        for earlier in range(b):
            count = count + jnp.where(ab_ref[earlier] == ab_ref[b], 1, 0)
        out.append(count)
    return out


def fill_factors(ab_ref, table):
    lane = lax.broadcasted_iota(jnp.int32, (SUB, LANES), 1)
    low = lane < ABLK
    rank = ranks(ab_ref)
    for t in range(2):
        own = jnp.where(low, ab_ref[2 * t], ab_ref[2 * t + 1])
        slot = jnp.where(low, rank[2 * t], rank[2 * t + 1])
        half = jnp.where(low, 0, 1)
        for label in range(LABELS):
            for kind, want in enumerate((half, 1 - half)):
                hit = jnp.where(own == label, jnp.where(slot == want, 1.0, 0.0), 0.0)
                table[(label * 2 + t) * KINDS + kind] = hit.astype(jnp.bfloat16)
            table[(label * 2 + t) * KINDS + 2] = jnp.where(own == label, 1.0, 0.0).astype(jnp.bfloat16)


def pack_kernel(cd_ref, ab_ref, place_ref, v_ref, o_ref, most_ref, table):
    fill_factors(ab_ref, table)
    most = jnp.int32(0)
    for count in ranks(ab_ref):
        most = jnp.maximum(most, count)
    most_ref[0] = most + 1
    subs = v_ref.shape[0] // SUB
    first = place_ref[0] * subs
    for j in range(subs):
        label = cd_ref[(first + j) // (KBLK // SUB)]
        straight = crossed = None
        for t in range(2):
            x = v_ref[j * SUB:(j + 1) * SUB, t * LANES:(t + 1) * LANES]
            at = (label * 2 + t) * KINDS
            s, c = x * table[at], x * table[at + 1]
            straight = s if straight is None else straight + s
            crossed = c if crossed is None else crossed + c
        o_ref[j * SUB:(j + 1) * SUB, :] = straight + swap_halves(crossed)


def pack(cd_irrep, ab_irrep, place, integrals):
    return pl.pallas_call(
        pack_kernel,
        out_shape=(
            jax.ShapeDtypeStruct((integrals.shape[0], LANES), jnp.bfloat16),
            jax.ShapeDtypeStruct((1,), jnp.int32),
        ),
        in_specs=[IN_SMEM, IN_SMEM, IN_SMEM, IN_VMEM],
        out_specs=(IN_VMEM, IN_SMEM),
        scratch_shapes=[TABLE],
        compiler_params=pltpu.CompilerParams(vmem_limit_bytes=2 * 2**20),
        cost_estimate=pl.CostEstimate(flops=10**10, bytes_accessed=2 * integrals.size, transcendentals=0),
        name="pack",
    )(cd_irrep, ab_irrep, place, integrals)


def half_ladder(dy, cd_ref, place_ref, table, piece_refs, held, masked):
    col = place_ref[0]
    core, z = lax.rem(col, 2), lax.rem(col // 2, 4)
    half = half_place(place_ref, dy)
    depth = piece_refs[0].shape[0]
    for n, ref in enumerate(piece_refs):
        dz = STEPS[n % 4]
        from_core = core if n < 4 else 1 - core
        at = (lax.rem(z + 4 - dz, 4) * 2 + from_core) * depth
        held[pl.ds(pl.multiple_of(at, SUB), depth), :] = ref[...]
    blocks = held.shape[0] // KBLK
    wide = held.shape[1] > LANES
    for blk in range(blocks):
        at = slice(blk * KBLK, (blk + 1) * KBLK)
        label = cd_ref[half * blocks + blk]
        for t in range(2):
            lanes = slice(t * LANES, (t + 1) * LANES)
            same, other, match = [jnp.concatenate([table[(label * 2 + t) * KINDS + kind]] * (KBLK // SUB), 0) for kind in range(3)]
            if wide:
                masked[at, lanes] = held[at, lanes] * match
            else:
                x = held[at, :]
                masked[at, lanes] = x * same + swap_halves(x) * other


def half_place(place_ref, dy):
    return lax.rem(place_ref[0] // 8 + dy, 2)


def half_product(dy, place_ref, t_ref, masked):
    depth = masked.shape[0]
    cols = pl.ds(pl.multiple_of(half_place(place_ref, dy) * depth, LANES), depth)
    return jnp.dot(t_ref[:, cols], masked[...], preferred_element_type=jnp.float32)


def first_kernel(cd_ref, ab_ref, place_ref, t_ref, *refs):
    piece_refs = refs[:8]
    o_ref, held, masked, table = refs[8:]
    fill_factors(ab_ref, table)
    half_ladder(0, cd_ref, place_ref, table, piece_refs, held, masked)
    o_ref[...] = half_product(0, place_ref, t_ref, masked)


def last_kernel(cd_ref, ab_ref, place_ref, t_ref, before_ref, *refs):
    piece_refs, out_refs = refs[:8], refs[8:16]
    held, masked, table, total = refs[16:]
    fill_factors(ab_ref, table)
    half_ladder(1, cd_ref, place_ref, table, piece_refs, held, masked)
    total[...] = (before_ref[...] + half_product(1, place_ref, t_ref, masked)).T
    row = place_ref[1]
    y, x = row // 4, lax.rem(row, 4)
    for (dy, dx), ref in zip(TARGETS, out_refs):
        target = lax.rem(y + dy, 2) * 4 + lax.rem(x + dx, 4)
        share = ref.shape[0]
        ref[...] = total[pl.ds(pl.multiple_of(target * share, 8), share), :]


TARGETS = [(0, 0), (1, 3), (1, 2), (1, 1), (1, 0), (0, 2), (0, 1), (0, 3)]


def row_hop(dy, dx):
    return [(i, (i // 4 ^ dy) * 4 + (i % 4 + dx) % 4) for i in range(8)]


def reduce_parts(blocks):
    parts = [blocks[0]]
    for n, block in enumerate(blocks[1:], 1):
        parts.append(lax.ppermute(block, "row", row_hop(*TARGETS[n])))
    return parts


STEPS = (0, 2, 1, 3)
CORE_SWAP = [(i, i ^ 1) for i in range(16)]


def hop(dy, dz):
    return [(i, ((i // 8 ^ dy) * 4 + (i // 2 + dz) % 4) * 2 + i % 2) for i in range(16)]


def partial_ladder(packed, amplitudes, cd_irrep, ab_irrep, place):
    across = lax.ppermute(packed, "col", hop(1, 0))
    pieces = []
    for start in (packed, across):
        mine = [start]
        for dz in STEPS[1:]:
            mine.append(lax.ppermute(start, "col", hop(0, dz)))
        theirs = []
        for dz, piece in zip(STEPS, mine):
            theirs.append(lax.ppermute(piece, "col", CORE_SWAP))
        pieces.append(mine + theirs)
    ij, cds = amplitudes.shape
    width, cols = 2 * LANES, cds // 2
    scratch = [VMEM((cols, packed.shape[1]), jnp.bfloat16), VMEM((cols, width), jnp.bfloat16), TABLE]
    cost = pl.CostEstimate(flops=ij * cds * width, bytes_accessed=ij * cds, transcendentals=0)
    limits = pltpu.CompilerParams(vmem_limit_bytes=12 * 2**20)
    half = pl.pallas_call(
        first_kernel,
        out_shape=jax.ShapeDtypeStruct((ij, width), jnp.float32),
        in_specs=[IN_SMEM] * 3 + [IN_VMEM] * 9,
        out_specs=IN_VMEM,
        scratch_shapes=scratch,
        compiler_params=limits,
        cost_estimate=cost,
        name="ladder_first",
    )(cd_irrep, ab_irrep, place, amplitudes, *pieces[0])
    return pl.pallas_call(
        last_kernel,
        out_shape=[jax.ShapeDtypeStruct((width // 8, ij), jnp.float32)] * 8,
        in_specs=[IN_SMEM] * 3 + [IN_VMEM] * 10,
        out_specs=[IN_VMEM] * 8,
        scratch_shapes=scratch + [VMEM((width, ij), jnp.float32)],
        compiler_params=limits,
        cost_estimate=cost,
        name="ladder_last",
    )(cd_irrep, ab_irrep, place, amplitudes, half, *pieces[1])


def shards(amplitudes, integrals, cd_irrep, ab_irrep, pair_energy, panel_energy):
    place = jnp.stack([lax.axis_index("col"), lax.axis_index("row")]).astype(jnp.int32)
    packed, most = pack(cd_irrep, ab_irrep, place, integrals)

    def narrow(packed, integrals, *rest):
        return partial_ladder(packed, *rest)

    def whole(packed, integrals, *rest):
        return partial_ladder(integrals, *rest)

    blocks = lax.cond(most[0] > 2, whole, narrow, packed, integrals, amplitudes, cd_irrep, ab_irrep, place)
    parts = reduce_parts(blocks)
    share = parts[0].shape[0]
    summed = sum(parts[1:], parts[0])
    energy_cols = lax.dynamic_slice_in_dim(panel_energy, lax.axis_index("row") * share, share, 0)
    denom = energy_cols[:, None] - pair_energy[None, :]
    return (summed / denom).astype(jnp.bfloat16).T


def solution(mesh):
    in_specs = (P("col", "row"), P(("row", "col"), None), P("row"), P(), P("col"), P())
    out_specs = P("col", "row")
    return jax.shard_map(shards, mesh=mesh, in_specs=in_specs, out_specs=out_specs, check_vma=False)
```

```python
import jax
import jax.numpy as jnp
from jax import lax
from jax.experimental import pallas as pl
from jax.experimental.pallas import tpu as pltpu
from jax.sharding import PartitionSpec as P


KBLK = 128
ABLK = 64
SUB = 16
LANES = 128
LABELS = 4
KINDS = 3
TABLE = pltpu.VMEM((LABELS * 2 * KINDS, SUB, LANES), jnp.bfloat16)
VMEM = pltpu.VMEM
SMEM = pltpu.SMEM
IN_SMEM = pl.BlockSpec(memory_space=SMEM)
IN_VMEM = pl.BlockSpec(memory_space=VMEM)


def swap_halves(x):
    return jnp.concatenate([x[:, ABLK:], x[:, :ABLK]], axis=1)


def ranks(ab_ref):
    out = []
    for b in range(4):
        count = jnp.int32(0)
        for earlier in range(b):
            count = count + jnp.where(ab_ref[earlier] == ab_ref[b], 1, 0)
        out.append(count)
    return out


def fill_factors(ab_ref, table):
    lane = lax.broadcasted_iota(jnp.int32, (SUB, LANES), 1)
    low = lane < ABLK
    rank = ranks(ab_ref)
    for t in range(2):
        own = jnp.where(low, ab_ref[2 * t], ab_ref[2 * t + 1])
        slot = jnp.where(low, rank[2 * t], rank[2 * t + 1])
        half = jnp.where(low, 0, 1)
        for label in range(LABELS):
            for kind, want in enumerate((half, 1 - half)):
                hit = jnp.where(own == label, jnp.where(slot == want, 1.0, 0.0), 0.0)
                table[(label * 2 + t) * KINDS + kind] = hit.astype(jnp.bfloat16)
            table[(label * 2 + t) * KINDS + 2] = jnp.where(own == label, 1.0, 0.0).astype(jnp.bfloat16)


def pack_kernel(cd_ref, ab_ref, place_ref, v_ref, o_ref, crowded_ref, table):
    fill_factors(ab_ref, table)
    most = jnp.int32(0)
    for count in ranks(ab_ref):
        most = jnp.maximum(most, count)
    crowded_ref[0] = jnp.where(most + 1 > 2, 1, 0)
    subs = v_ref.shape[0] // SUB
    first = place_ref[0] * subs
    for j in range(subs):
        label = cd_ref[(first + j) // (KBLK // SUB)]
        straight = crossed = None
        for t in range(2):
            x = v_ref[j * SUB:(j + 1) * SUB, t * LANES:(t + 1) * LANES]
            at = (label * 2 + t) * KINDS
            s, c = x * table[at], x * table[at + 1]
            straight = s if straight is None else straight + s
            crossed = c if crossed is None else crossed + c
        o_ref[j * SUB:(j + 1) * SUB, :] = straight + swap_halves(crossed)


def pack(cd_irrep, ab_irrep, place, integrals):
    return pl.pallas_call(
        pack_kernel,
        out_shape=(
            jax.ShapeDtypeStruct((integrals.shape[0], LANES), jnp.bfloat16),
            jax.ShapeDtypeStruct((1,), jnp.int32),
        ),
        in_specs=[IN_SMEM, IN_SMEM, IN_SMEM, IN_VMEM],
        out_specs=(IN_VMEM, IN_SMEM),
        scratch_shapes=[TABLE],
        compiler_params=pltpu.CompilerParams(vmem_limit_bytes=2 * 2**20),
        cost_estimate=pl.CostEstimate(flops=10**10, bytes_accessed=2 * integrals.size, transcendentals=0),
        name="pack",
    )(cd_irrep, ab_irrep, place, integrals)


def half_ladder(dy, cd_ref, place_ref, table, piece_refs, held, masked):
    col = place_ref[0]
    core, z = lax.rem(col, 2), lax.rem(col // 2, 4)
    half = half_place(place_ref, dy)
    depth = piece_refs[0].shape[0]
    for n, ref in enumerate(piece_refs):
        dz = STEPS[n % 4]
        from_core = core if n < 4 else 1 - core
        at = (lax.rem(z + 4 - dz, 4) * 2 + from_core) * depth
        held[pl.ds(pl.multiple_of(at, SUB), depth), :] = ref[...]
    blocks = held.shape[0] // KBLK
    wide = held.shape[1] > LANES
    for blk in range(blocks):
        at = slice(blk * KBLK, (blk + 1) * KBLK)
        label = cd_ref[half * blocks + blk]
        for t in range(2):
            lanes = slice(t * LANES, (t + 1) * LANES)
            same, other, match = [jnp.concatenate([table[(label * 2 + t) * KINDS + kind]] * (KBLK // SUB), 0) for kind in range(3)]
            if wide:
                masked[at, lanes] = held[at, lanes] * match
            else:
                x = held[at, :]
                masked[at, lanes] = x * same + swap_halves(x) * other


def half_place(place_ref, dy):
    return lax.rem(place_ref[0] // 8 + dy, 2)


def half_product(dy, place_ref, t_ref, masked):
    depth = masked.shape[0]
    cols = pl.ds(pl.multiple_of(half_place(place_ref, dy) * depth, LANES), depth)
    return jnp.dot(t_ref[:, cols], masked[...], preferred_element_type=jnp.float32)


def first_kernel(cd_ref, ab_ref, place_ref, t_ref, *refs):
    piece_refs = refs[:8]
    o_ref, held, masked, table = refs[8:]
    fill_factors(ab_ref, table)
    half_ladder(0, cd_ref, place_ref, table, piece_refs, held, masked)
    o_ref[...] = half_product(0, place_ref, t_ref, masked)


def last_kernel(cd_ref, ab_ref, place_ref, t_ref, before_ref, *refs):
    piece_refs, out_refs = refs[:8], refs[8:16]
    held, masked, table, total = refs[16:]
    fill_factors(ab_ref, table)
    half_ladder(1, cd_ref, place_ref, table, piece_refs, held, masked)
    total[...] = (before_ref[...] + half_product(1, place_ref, t_ref, masked)).T
    row = place_ref[1]
    y, x = row // 4, lax.rem(row, 4)
    for (dy, dx), ref in zip(TARGETS, out_refs):
        target = lax.rem(y + dy, 2) * 4 + lax.rem(x + dx, 4)
        share = ref.shape[0]
        ref[...] = total[pl.ds(pl.multiple_of(target * share, 8), share), :]


TARGETS = [(0, 0), (0, 2), (1, 3), (1, 2), (1, 1), (1, 0), (0, 1), (0, 3)]


def row_hop(dy, dx):
    return [(i, (i // 4 ^ dy) * 4 + (i % 4 + dx) % 4) for i in range(8)]


def reduce_parts(blocks):
    parts = [blocks[0]]
    for n, block in enumerate(blocks[1:], 1):
        parts.append(lax.ppermute(block, "row", row_hop(*TARGETS[n])))
    return parts


STEPS = (0, 2, 1, 3)
CORE_SWAP = [(i, i ^ 1) for i in range(16)]


def hop(dy, dz):
    return [(i, ((i // 8 ^ dy) * 4 + (i // 2 + dz) % 4) * 2 + i % 2) for i in range(16)]


def partial_ladder(packed, amplitudes, cd_irrep, ab_irrep, place):
    across = lax.ppermute(packed, "col", hop(1, 0))
    pieces = []
    for start in (packed, across):
        mine = [start]
        for dz in STEPS[1:]:
            mine.append(lax.ppermute(start, "col", hop(0, dz)))
        theirs = []
        for dz, piece in zip(STEPS, mine):
            theirs.append(lax.ppermute(piece, "col", CORE_SWAP))
        pieces.append(mine + theirs)
    ij, cds = amplitudes.shape
    width, cols = 2 * LANES, cds // 2
    scratch = [VMEM((cols, packed.shape[1]), jnp.bfloat16), VMEM((cols, width), jnp.bfloat16), TABLE]
    cost = pl.CostEstimate(flops=ij * cds * width, bytes_accessed=ij * cds, transcendentals=0)
    limits = pltpu.CompilerParams(vmem_limit_bytes=12 * 2**20)
    half = pl.pallas_call(
        first_kernel,
        out_shape=jax.ShapeDtypeStruct((ij, width), jnp.float32),
        in_specs=[IN_SMEM] * 3 + [IN_VMEM] * 9,
        out_specs=IN_VMEM,
        scratch_shapes=scratch,
        compiler_params=limits,
        cost_estimate=cost,
        name="ladder_first",
    )(cd_irrep, ab_irrep, place, amplitudes, *pieces[0])
    return pl.pallas_call(
        last_kernel,
        out_shape=[jax.ShapeDtypeStruct((width // 8, ij), jnp.float32)] * 8,
        in_specs=[IN_SMEM] * 3 + [IN_VMEM] * 10,
        out_specs=[IN_VMEM] * 8,
        scratch_shapes=scratch + [VMEM((width, ij), jnp.float32)],
        compiler_params=limits,
        cost_estimate=cost,
        name="ladder_last",
    )(cd_irrep, ab_irrep, place, amplitudes, half, *pieces[1])


def shards(amplitudes, integrals, cd_irrep, ab_irrep, pair_energy, panel_energy):
    place = jnp.stack([lax.axis_index("col"), lax.axis_index("row")]).astype(jnp.int32)
    packed, crowded = pack(cd_irrep, ab_irrep, place, integrals)

    def narrow(packed, integrals, *rest):
        return partial_ladder(packed, *rest)

    def whole(packed, integrals, *rest):
        return partial_ladder(integrals, *rest)

    blocks = lax.switch(crowded[0], (narrow, whole), packed, integrals, amplitudes, cd_irrep, ab_irrep, place)
    parts = reduce_parts(blocks)
    share = parts[0].shape[0]
    summed = sum(parts[1:], parts[0])
    energy_cols = lax.dynamic_slice_in_dim(panel_energy, lax.axis_index("row") * share, share, 0)
    denom = energy_cols[:, None] - pair_energy[None, :]
    return (summed / denom).astype(jnp.bfloat16).T


def solution(mesh):
    in_specs = (P("col", "row"), P(("row", "col"), None), P("row"), P(), P("col"), P())
    out_specs = P("col", "row")
    return jax.shard_map(shards, mesh=mesh, in_specs=in_specs, out_specs=out_specs, check_vma=False)
```
